32 devices in a mesh: outer: 8 (over z, x), inner: 4 (over y, core).
Axes of the slice: x: 2, y: 2, z: 4, core: 2. Of those that a mesh axis runs over, the one named last changes fastest.
Arguments:
- fine_input: bfloat16 [6144, 2048], P(('outer', 'inner')), may hold values from -12 to 12
- fine_query: bfloat16 [6144, 1024], P(('outer', 'inner')), may hold values from -4.5 to 4.5
- fine_key: bfloat16 [6144, 1024], P(('outer', 'inner')), may hold values from -4.5 to 4.5
- fine_value: bfloat16 [6144, 1024], P(('outer', 'inner')), may hold values from -6 to 6
- w_fine_out: bfloat16 [1024, 2048], P(None, 'inner'), may hold values from -0.1875 to 0.1875
- norm_gain: float32 [2048], replicated, may hold values from 0.25 to 1.75
- w_query: bfloat16 [2048, 512], P(None, 'inner'), may hold values from -1 to 1
- w_key: bfloat16 [2048, 512], P(None, 'inner'), may hold values from -1 to 1
- w_value: bfloat16 [2048, 512], P(None, 'inner'), may hold values from -0.125 to 0.125
- w_coarse_out: bfloat16 [512, 2048], P('inner'), may hold values from -0.25 to 0.25
Outputs:
- mixed_stream: bfloat16 [6144, 2048], P(('outer', 'inner'))
The draws below stay inside these ranges and needn't reach their ends.
All inputs are finite; a program needn't handle non-finite values.
Results may differ from the reference program's by a relative error of at most 0.008.
Values may be sent and summed in bfloat16 or wider, within the bound.
No kernel may reach another device: no remote copies, remote signals or barrier semaphores. Data moves between devices by JAX's collectives and lax.ppermute only.
A program may use at most 128 MiB of HBM per device.

```python
import math
import jax
import jax.numpy as jnp
from jax import lax

D = 2048
HE = 128
HF = 8
WIN = 512
POOL = 8
TOKENS = 6144
LC = 768
HC = 4


def draw_fine_input(key, part):
    stream = jnp.clip(jax.random.normal(jax.random.fold_in(key, 7301), (TOKENS, D), jnp.float32), -6.0, 6.0)
    return stream.astype(jnp.bfloat16)


def draw_fine_query(key, part):
    noise = jnp.clip(jax.random.normal(jax.random.fold_in(key, 7101), (TOKENS, HF * HE), jnp.float32), -4.5, 4.5)
    return noise.astype(jnp.bfloat16)


def draw_fine_key(key, part):
    noise = jnp.clip(jax.random.normal(jax.random.fold_in(key, 7102), (TOKENS, HF * HE), jnp.float32), -4.5, 4.5)
    return noise.astype(jnp.bfloat16)


def projection_draw(key, salt, spread):
    matrix = spread * jnp.clip(jax.random.normal(jax.random.fold_in(key, salt), (D, HC * HE), jnp.float32), -4.0, 4.0) / math.sqrt(D)
    return jnp.clip(matrix, -1.0, 1.0).astype(jnp.bfloat16)


def draw_w_query(key, part):
    spread = 2.0
    return projection_draw(key, 7401, spread)


def draw_w_key(key, part):
    return projection_draw(key, 7402, 1.0)


def steps_of(key, dims, cuts, smallest, top_value):
    factor_of, own = 1.0, jax.random.fold_in(key, 6)
    for axis_at, blocks in cuts:
        heights = jnp.exp(jax.random.uniform(jax.random.fold_in(own, axis_at), (blocks,), jnp.float32, smallest / len(cuts), top_value / len(cuts)))
        factor_of = factor_of * jnp.repeat(heights, dims[axis_at] // blocks).reshape([-1 if axis == axis_at else 1 for axis in range(len(dims))])
    return factor_of


def normal_values(rng, extent, scale, most, shards=(), kind=jnp.bfloat16):
    result = scale * jax.random.normal(rng, extent, jnp.float32)
    if shards:
        result = result * steps_of(rng, extent, shards, -0.22, 0.18)
    return jnp.clip(result, -most, most).astype(kind)


def setup_inputs(seed: int = 0) -> dict:
    streams_of = jax.random.split(jax.random.key(seed), 11)
    return {
        "fine_input": draw_fine_input(jax.random.fold_in(streams_of[10], 71), 0),
        "fine_query": draw_fine_query(jax.random.fold_in(streams_of[10], 71), 0),
        "fine_key": draw_fine_key(jax.random.fold_in(streams_of[10], 71), 0),
        "fine_value": normal_values(streams_of[3], (TOKENS, HF * HE), 1.0, 6.0, ((0, 32),)),
        "w_fine_out": normal_values(streams_of[4], (HF * HE, D), (HF * HE) ** -0.5, 0.1875, ((1, 4),)),
        "norm_gain": jnp.clip(1.0 + 0.15 * jax.random.normal(streams_of[5], (D,), jnp.float32), 0.25, 1.75),
        "w_query": draw_w_query(jax.random.fold_in(streams_of[10], 71), 0),
        "w_key": draw_w_key(jax.random.fold_in(streams_of[10], 71), 0),
        "w_value": normal_values(streams_of[8], (D, HC * HE), D ** -0.5, 0.125, ((1, 4),)),
        "w_coarse_out": normal_values(streams_of[9], (HC * HE, D), (HC * HE) ** -0.5, 0.25, ((0, 4),)),
    }


very_negative = -1e+30

def softmax_mix(scores, allowed, values):
    masked = jnp.where(allowed, scores, very_negative)
    row_max = lax.optimization_barrier(jnp.max(masked, axis=-1, keepdims=True))
    exp_weights = jnp.where(allowed, jnp.exp(scores - row_max), 0.0)
    row_sum = lax.optimization_barrier(jnp.sum(exp_weights, axis=-1))
    rounded = lax.optimization_barrier(exp_weights.astype(jnp.bfloat16)).astype(jnp.float32)
    summed = jnp.einsum('hqk,khe->qhe', rounded, values.astype(jnp.float32))
    return (summed / jnp.transpose(row_sum)[:, :, None]).astype(jnp.bfloat16)

def fine_attention(fine_query, fine_key, fine_value):
    head_count = fine_query.shape[1] // HE
    score_scale = 1.0 / math.sqrt(HE)
    query_heads = fine_query.reshape(TOKENS, head_count, HE)
    padding = jnp.zeros((WIN, head_count * HE), jnp.bfloat16)
    key_heads = jnp.concatenate([padding, fine_key], axis=0).reshape(TOKENS + WIN, head_count, HE)
    value_heads = jnp.concatenate([padding, fine_value], axis=0).reshape(TOKENS + WIN, head_count, HE)
    row_ids = jnp.arange(WIN, dtype=jnp.int32)[:, None] + WIN
    col_ids = jnp.arange(2 * WIN, dtype=jnp.int32)[None, :]
    distance = row_ids - col_ids

    def one_block(number):
        first_row = (number * WIN).astype(jnp.int32)
        block_query = lax.dynamic_slice_in_dim(query_heads, first_row, WIN, 0)
        block_key = lax.dynamic_slice_in_dim(key_heads, first_row, 2 * WIN, 0)
        block_value = lax.dynamic_slice_in_dim(value_heads, first_row, 2 * WIN, 0)
        scores = jnp.einsum('qhe,khe->hqk', block_query.astype(jnp.float32), block_key.astype(jnp.float32)) * score_scale
        allowed = (distance >= 0) & (distance < WIN) & (first_row + col_ids >= WIN)
        return softmax_mix(scores, allowed[None], block_value)
    mixed = lax.map(one_block, jnp.arange(TOKENS // WIN, dtype=jnp.int32))
    return mixed.reshape(TOKENS, head_count * HE)

def coarse_attention(coarse_query, coarse_key, coarse_value):
    head_count = coarse_query.shape[1] // HE
    score_scale = 1.0 / math.sqrt(HE)
    block_size = math.gcd(LC, 256)
    query_heads = coarse_query.reshape(LC, head_count, HE)
    key_heads = coarse_key.reshape(LC, head_count, HE)
    value_heads = coarse_value.reshape(LC, head_count, HE)
    col_ids = jnp.arange(LC, dtype=jnp.int32)[None, :]

    def one_block(number):
        first_row = (number * block_size).astype(jnp.int32)
        block_query = lax.dynamic_slice_in_dim(query_heads, first_row, block_size, 0)
        scores = jnp.einsum('qhe,khe->hqk', block_query.astype(jnp.float32), key_heads.astype(jnp.float32)) * score_scale
        row_ids = first_row + jnp.arange(block_size, dtype=jnp.int32)[:, None]
        allowed = col_ids <= row_ids
        return softmax_mix(scores, allowed[None], value_heads)
    mixed = lax.map(one_block, jnp.arange(LC // block_size, dtype=jnp.int32))
    return mixed.reshape(LC, head_count * HE)

def reference(fine_input, fine_query, fine_key, fine_value, w_fine_out, norm_gain, w_query, w_key, w_value, w_coarse_out):
    fine_mix = fine_attention(fine_query, fine_key, fine_value)
    fine_state = (fine_input.astype(jnp.float32) + jnp.dot(fine_mix, w_fine_out, preferred_element_type=jnp.float32)).astype(jnp.bfloat16)
    shifted = jnp.concatenate([jnp.zeros((POOL - 1, D), jnp.bfloat16), fine_state[:TOKENS - POOL + 1]], axis=0)
    pooled = (lax.optimization_barrier(jnp.sum(shifted.reshape(LC, POOL, D).astype(jnp.float32), axis=1)) / POOL).astype(jnp.bfloat16)
    pooled_wide = pooled.astype(jnp.float32)
    moment = lax.optimization_barrier(jnp.mean(pooled_wide * pooled_wide, axis=-1, keepdims=True))
    normed = (pooled_wide * lax.rsqrt(moment + 1e-06) * norm_gain).astype(jnp.bfloat16)
    coarse_query = jnp.dot(normed, w_query, preferred_element_type=jnp.float32).astype(jnp.bfloat16)
    coarse_key = jnp.dot(normed, w_key, preferred_element_type=jnp.float32).astype(jnp.bfloat16)
    coarse_value = jnp.dot(normed, w_value, preferred_element_type=jnp.float32).astype(jnp.bfloat16)
    coarse_mix = coarse_attention(coarse_query, coarse_key, coarse_value)
    coarse_out = (pooled_wide + jnp.dot(coarse_mix, w_coarse_out, preferred_element_type=jnp.float32)).astype(jnp.bfloat16)
    lifted = jnp.repeat(coarse_out, POOL, axis=0)
    return (fine_state.astype(jnp.float32) + lifted.astype(jnp.float32)).astype(jnp.bfloat16)
```

```python
import math

import jax
import jax.numpy as jnp
from jax import lax
from jax.sharding import PartitionSpec as P

HE = 128
WIN = 512
POOL = 8


very_negative = -1e30


def passed_along(block, axis, distance):
    devices = range(lax.axis_size(axis))
    route = [(i - distance, i) for i in devices if i - distance in devices]
    return lax.ppermute(block, axis, route)


def swapped_cores(block):
    count = lax.axis_size("inner")
    return lax.ppermute(block, "inner", [(i, i ^ 1) for i in range(count)])


def columns_of_all(shard):
    count = lax.axis_size("inner")
    me = lax.axis_index("inner")
    rows, width = shard.shape
    joined = jnp.zeros((rows, count * width), shard.dtype)
    for hop in range(0, count, 2):
        near = shard
        if hop:
            near = lax.ppermute(shard, "inner", [(i, (i + hop) % count) for i in range(count)])
        owner = (me - hop) % count
        joined = lax.dynamic_update_slice(joined, near, (0, owner * width))
        joined = lax.dynamic_update_slice(joined, swapped_cores(near), (0, (owner ^ 1) * width))
    return joined


def outer_gather(block):
    count = lax.axis_size("outer")
    pairs = [[i, i + 1] for i in range(0, count, 2)]
    lines = [list(range(i, count, 2)) for i in range(2)]
    near = lax.all_gather(block, "outer", axis=0, tiled=True, axis_index_groups=pairs)
    return lax.all_gather(near, "outer", axis=0, tiled=True, axis_index_groups=lines)


def summed_pieces(block):
    count = lax.axis_size("inner")
    me = lax.axis_index("inner")
    parts = block.reshape(count, block.shape[0] // count, block.shape[1])
    own = lax.dynamic_index_in_dim(parts, me, 0, keepdims=False).astype(jnp.float32)
    for hop in range(1, count):
        piece = lax.dynamic_index_in_dim(parts, me ^ hop, 0, keepdims=False)
        own = own + lax.ppermute(piece, "inner", [(i, i ^ hop) for i in range(count)]).astype(
            jnp.float32
        )
    return own


def on_device(
    fine_input,
    fine_query,
    fine_key,
    fine_value,
    w_fine_out,
    norm_gain,
    w_query,
    w_key,
    w_value,
    w_coarse_out,
):
    tok_rows, model_width = fine_input.shape
    fine_heads = fine_query.shape[1] // HE
    score_scale = 1.0 / math.sqrt(HE)
    reach_count = (WIN + tok_rows - 1) // tok_rows
    position = lax.axis_index(("outer", "inner"))
    fine_width = fine_key.shape[1]
    joined_kv = jnp.concatenate([fine_key, fine_value], axis=1)
    far_rows = -(-(WIN - (reach_count - 1) * tok_rows) // 16) * 16
    pieces_kv = []
    for distance in range(reach_count, 0, -1):
        first = tok_rows - far_rows if distance == reach_count else 0
        pieces_kv.append(passed_along(joined_kv[first:], ("outer", "inner"), distance))
    pieces_kv.append(joined_kv)
    span = reach_count * tok_rows + far_rows
    all_kv = jnp.concatenate(pieces_kv, axis=0)
    key_heads = all_kv[:, :fine_width].reshape(span, fine_heads, HE)
    value_heads = all_kv[:, fine_width:].reshape(span, fine_heads, HE)
    query_heads = fine_query.reshape(tok_rows, fine_heads, HE)
    scores = (
        jnp.einsum("qhe,khe->hqk", query_heads, key_heads, preferred_element_type=jnp.float32)
        * score_scale
    )
    row_ids = jnp.arange(tok_rows, dtype=jnp.int32)[:, None] + span - tok_rows
    col_ids = jnp.arange(span, dtype=jnp.int32)[None, :]
    gap_rows = row_ids - col_ids
    allowed = (
        (gap_rows >= 0) & (gap_rows < WIN) & (position * tok_rows - (span - tok_rows) + col_ids >= 0)
    )
    masked = jnp.where(allowed[None], scores, very_negative)
    row_max = jnp.max(masked, axis=-1, keepdims=True)
    exp_weights = jnp.where(allowed[None], jnp.exp(scores - row_max), 0.0)
    row_sum = jnp.sum(exp_weights, axis=-1)
    summed = jnp.einsum(
        "hqk,khe->qhe",
        exp_weights.astype(jnp.bfloat16),
        value_heads,
        preferred_element_type=jnp.float32,
    )
    fine_mix = (
        (summed / jnp.transpose(row_sum)[:, :, None])
        .astype(jnp.bfloat16)
        .reshape(tok_rows, fine_heads * HE)
    )
    projected = jnp.dot(
        fine_mix,
        columns_of_all(w_fine_out),
        preferred_element_type=jnp.float32,
    )
    fine_state = (fine_input.astype(jnp.float32) + projected).astype(jnp.bfloat16)
    edge_rows = passed_along(fine_state[tok_rows - POOL + 1 :], ("outer", "inner"), 1)
    first_pool = (
        jnp.sum(edge_rows, axis=0, dtype=jnp.float32) + fine_state[0].astype(jnp.float32)
    ) / POOL
    later_pools = (
        jnp.sum(
            fine_state[1 : tok_rows - POOL + 1].reshape(tok_rows // POOL - 1, POOL, model_width),
            axis=1,
            dtype=jnp.float32,
        )
        / POOL
    )
    pooled = jnp.concatenate([first_pool[None], later_pools], axis=0).astype(jnp.bfloat16)
    pooled_wide = pooled.astype(jnp.float32)
    moment = jnp.mean(pooled_wide * pooled_wide, axis=-1, keepdims=True)
    normed = (pooled_wide * lax.rsqrt(moment + 1e-06) * norm_gain).astype(jnp.bfloat16)
    local_heads = w_query.shape[1] // HE
    head_width = local_heads * HE
    joined_weights = jnp.concatenate([w_query, w_key, w_value], axis=1)
    projections = jnp.dot(
        lax.all_gather(normed, "inner", axis=0, tiled=True),
        joined_weights,
        preferred_element_type=jnp.float32,
    ).astype(jnp.bfloat16)
    group_len = projections.shape[0]
    coarse_query = projections[:, :head_width].reshape(group_len, local_heads, HE)
    outer_index = lax.axis_index("outer")
    query_pos = outer_index * group_len + jnp.arange(group_len, dtype=jnp.int32)
    gathered = outer_gather(projections[:, head_width:])
    pieces = (gathered[:, :head_width], gathered[:, head_width:])
    prior_max = jnp.full((local_heads, group_len), very_negative, jnp.float32)
    count = pieces[0].shape[0]
    block_keys = pieces[0].reshape(count, local_heads, HE)
    block_values = pieces[1].reshape(count, local_heads, HE)
    block_scores = (
        jnp.einsum("qhe,khe->hqk", coarse_query, block_keys, preferred_element_type=jnp.float32)
        * score_scale
    )
    key_pos = jnp.arange(count, dtype=jnp.int32)
    visible = (key_pos[None, :] <= query_pos[:, None])[None]
    block_masked = jnp.where(visible, block_scores, very_negative)
    new_max = jnp.maximum(prior_max, jnp.max(block_masked, axis=-1))
    block_exp = jnp.where(visible, jnp.exp(block_scores - new_max[:, :, None]), 0.0)
    new_sum = jnp.sum(block_exp, axis=-1)
    contrib = jnp.einsum(
        "hqk,khe->hqe",
        block_exp.astype(jnp.bfloat16),
        block_values,
        preferred_element_type=jnp.float32,
    )
    coarse_mix = (
        jnp.transpose(contrib / new_sum[:, :, None], (1, 0, 2))
        .reshape(group_len, head_width)
        .astype(jnp.bfloat16)
    )
    head_total = summed_pieces(
        jnp.dot(coarse_mix, w_coarse_out, preferred_element_type=jnp.float32).astype(jnp.bfloat16)
    )
    coarse_out = (pooled_wide + head_total).astype(jnp.bfloat16)
    fine_groups = fine_state.reshape(tok_rows // POOL, POOL, model_width).astype(jnp.float32)
    lifted = fine_groups + coarse_out.astype(jnp.float32)[:, None, :]
    return lifted.reshape(tok_rows, model_width).astype(jnp.bfloat16)


def solution(mesh):
    placed = (
        P(("outer", "inner"), None),
        P(("outer", "inner"), None),
        P(("outer", "inner"), None),
        P(("outer", "inner"), None),
        P(None, "inner"),
        P(),
        P(None, "inner"),
        P(None, "inner"),
        P(None, "inner"),
        P("inner", None),
    )
    return jax.shard_map(
        on_device,
        mesh=mesh,
        in_specs=placed,
        out_specs=P(("outer", "inner"), None),
        check_vma=False,
    )
```

```python
import functools
import math

import jax
import jax.numpy as jnp
from jax import lax
from jax.experimental import pallas as pl
from jax.experimental.pallas import tpu as pltpu
from jax.sharding import PartitionSpec as P

HE = 128
WIN = 512
POOL = 8
EXTRA = 16
BOTH = ("outer", "inner")

very_negative = -1e30


def on_ahead(block, distance):
    count = lax.axis_size(BOTH)
    return lax.ppermute(block, BOTH, [(i, i + distance) for i in range(count - distance)])


def swapped_cores(block):
    count = lax.axis_size("inner")
    return lax.ppermute(block, "inner", [(i, i ^ 1) for i in range(count)])


def outer_mate(outer, inner):
    return outer ^ (1 if (inner >> 1) % 2 == 0 else 2)


def mate_bit(outer, inner):
    return jnp.where((inner >> 1) % 2 == 0, outer % 2, (outer >> 1) % 2)


def shards_of_all(shard):
    count, blocks = lax.axis_size("inner"), lax.axis_size("outer")
    me, outer = lax.axis_index("inner"), lax.axis_index("outer")
    half = shard.shape[0] // 2
    mates = [
        (o * count + i, outer_mate(o, i) * count + i) for o in range(blocks) for i in range(count)
    ]
    fetched = []
    for hop in range(2, count, 2):
        wanted = mate_bit(outer, (me + hop) % count)
        part = lax.dynamic_slice_in_dim(shard, wanted * half, half, 0)
        near = lax.ppermute(part, "inner", [(i, (i + hop) % count) for i in range(count)])
        fetched.append((near, lax.ppermute(near, BOTH, mates)))
    pieces = [shard, swapped_cores(shard)]
    for near, far in fetched:
        pieces += [near, far, swapped_cores(near), swapped_cores(far)]
    return pieces


def outer_gather(block):
    count = lax.axis_size("outer")
    pairs = [[i, i + 1] for i in range(0, count, 2)]
    lines = [list(range(i, count, 2)) for i in range(2)]
    near = lax.all_gather(block, "outer", axis=0, tiled=True, axis_index_groups=pairs)
    return lax.all_gather(near, "outer", axis=0, tiled=True, axis_index_groups=lines)


def summed_pieces(block):
    count = lax.axis_size("inner")
    me = lax.axis_index("inner")
    parts = block.reshape(count, block.shape[0] // count, block.shape[1])
    own = lax.dynamic_index_in_dim(parts, me, 0, keepdims=False).astype(jnp.float32)
    for hop in range(1, count):
        piece = lax.dynamic_index_in_dim(parts, me ^ hop, 0, keepdims=False)
        own = own + lax.ppermute(piece, "inner", [(i, i ^ hop) for i in range(count)]).astype(
            jnp.float32
        )
    return own


def attention_kernel(takes, query, key, value, mate, *refs):
    halos = refs[: len(takes)]
    mine_out, send_out, q_all, k_all, v_all, bias, sems = refs[len(takes) :]
    rows = query.shape[0]
    width = q_all.shape[1]
    core = lax.axis_index("inner") % 2
    chip = (lax.axis_index("outer") * lax.axis_size("inner") + lax.axis_index("inner")) // 2
    halo = sum(takes)
    copies = []

    def place(source, target):
        copy = pltpu.make_async_copy(source, target, sems.at[len(copies)])
        copy.start()
        copies.append(copy)

    own = pl.multiple_of(core * rows, 16)
    other = pl.multiple_of((1 - core) * rows, 16)
    columns = pl.ds(pl.multiple_of(core * width, 128), width)
    place(query.at[:, columns], q_all.at[pl.ds(EXTRA + own, rows)])
    place(key.at[:, columns], k_all.at[pl.ds(halo + own, rows)])
    place(value.at[:, columns], v_all.at[pl.ds(halo + own, rows)])
    place(mate.at[:, pl.ds(0, width)], q_all.at[pl.ds(EXTRA + other, rows)])
    place(mate.at[:, pl.ds(width, width)], k_all.at[pl.ds(halo + other, rows)])
    place(mate.at[:, pl.ds(2 * width, width)], v_all.at[pl.ds(halo + other, rows)])
    place(halos[0].at[pl.ds(takes[0], EXTRA), pl.ds(0, width)], q_all.at[pl.ds(0, EXTRA)])
    start = halo
    for take, ref in zip(takes, halos):
        start -= take
        place(ref.at[pl.ds(0, take), pl.ds(0, width)], k_all.at[pl.ds(start, take)])
        place(ref.at[pl.ds(0, take), pl.ds(width, width)], v_all.at[pl.ds(start, take)])

    count, span = mine_out.shape[0], halo + rows
    row = lax.broadcasted_iota(jnp.int32, (count, span), 0) - EXTRA
    col = lax.broadcasted_iota(jnp.int32, (count, span), 1) - halo
    gap = row - col
    near = (gap >= 0) & (gap < WIN)
    scale = 1.0 / math.sqrt(HE)
    for copy in copies:
        copy.wait()
    for which, out in ((1 - core, send_out), (core, mine_out)):
        first = pl.multiple_of(which * rows, 16)
        bias[...] = jnp.where(near & (col + chip * 2 * rows + first >= 0), 0.0, very_negative)
        for head in range(width // HE):
            lanes = pl.ds(head * HE, HE)
            scores = lax.dot_general(
                q_all[pl.ds(first, count), lanes],
                k_all[pl.ds(first, span), lanes],
                (((1,), (1,)), ((), ())),
                preferred_element_type=jnp.float32,
            )
            masked = scores * scale + bias[...]
            top = jnp.max(masked, axis=-1, keepdims=True)
            weights = jnp.exp(masked - top)
            total = jnp.sum(weights, axis=-1, keepdims=True)
            summed = jnp.dot(
                weights.astype(jnp.bfloat16),
                v_all[pl.ds(first, span), lanes],
                preferred_element_type=jnp.float32,
            )
            out[:, lanes] = (summed / total).astype(jnp.bfloat16)


def fine_attention(fine_query, fine_key, fine_value):
    rows, full = fine_query.shape
    width = full // 2
    core = lax.axis_index("inner") % 2
    away = (1 - core) * width
    kept = core * width
    parts = (fine_query, fine_key, fine_value)
    mate = swapped_cores(
        jnp.concatenate([lax.dynamic_slice_in_dim(a, away, width, 1) for a in parts], axis=1)
    )
    mine = jnp.concatenate([lax.dynamic_slice_in_dim(a, kept, width, 1) for a in parts], axis=1)
    low = jnp.where(core == 0, mine, mate)
    high = jnp.where(core == 0, mate, mine)
    left = -(-(WIN - 1 + EXTRA) // 16) * 16
    takes = []
    while left > 0:
        takes.append(min(left, 2 * rows))
        left -= takes[-1]
    chip_kv = jnp.concatenate([low[:, width:], high[:, width:]], axis=0)
    halos = []
    for at, take in enumerate(takes):
        block = chip_kv[2 * rows - take :]
        if at == 0:
            edge = jnp.pad(high[rows - EXTRA :, :width], ((0, 0), (0, width)))
            block = jnp.concatenate([block, edge], axis=0)
        halos.append(on_ahead(block, 2 * (at + 1)))
    count, halo = rows + EXTRA, sum(takes)
    anywhere = pl.BlockSpec(memory_space=pl.ANY)
    out = jax.ShapeDtypeStruct((count, width), jnp.bfloat16)
    pairs = 4 * (width // HE) * count * (halo + rows)
    return pl.pallas_call(
        functools.partial(attention_kernel, tuple(takes)),
        out_shape=(out, out),
        in_specs=[anywhere] * (4 + len(takes)),
        out_specs=(pl.BlockSpec(memory_space=pltpu.VMEM),) * 2,
        scratch_shapes=[
            pltpu.VMEM((2 * rows + EXTRA, width), jnp.bfloat16),
            pltpu.VMEM((2 * rows + halo, width), jnp.bfloat16),
            pltpu.VMEM((2 * rows + halo, width), jnp.bfloat16),
            pltpu.VMEM((count, halo + rows), jnp.float32),
            pltpu.SemaphoreType.DMA((7 + 2 * len(takes),)),
        ],
        compiler_params=pltpu.CompilerParams(vmem_limit_bytes=24 * 1024 * 1024),
        cost_estimate=pl.CostEstimate(
            flops=2 * pairs * HE, bytes_accessed=6 * rows * full, transcendentals=pairs // 2
        ),
        name="fine_attention",
    )(fine_query, fine_key, fine_value, mate, *halos)


def state_kernel(counts, mix_mine, mix_mate, stream, edge, gain, *refs):
    pieces, refs = refs[: counts[0]], refs[counts[0] :]
    state_out, pooled_out, normed_out, mix, weights, wide, sems = refs
    rows, model_width = stream.shape
    devices = lax.axis_size("inner")
    shard = model_width // devices
    depth, half = weights.shape[1], weights.shape[1] // 2
    me, outer = lax.axis_index("inner"), lax.axis_index("outer")
    core = me % 2
    bit = jnp.where((me // 2) % 2 == 0, outer % 2, (outer // 2) % 2)
    first_half = pl.ds(pl.multiple_of(bit * half, 16), half)
    second_half = pl.ds(pl.multiple_of((1 - bit) * half, 16), half)
    slots = [[(pieces[0], None)], [(pieces[1], None)]]
    owners = [me, me + 1 - 2 * core]
    for hop in range(2, devices, 2):
        near, far, near_mate, far_mate = pieces[2 * hop - 2 : 2 * hop + 2]
        owner = lax.rem(me - hop + devices, devices)
        slots += [
            [(near, first_half), (far, second_half)],
            [(near_mate, first_half), (far_mate, second_half)],
        ]
        owners += [owner, owner + 1 - 2 * core]
    copies = []
    for slot, parts in enumerate(slots):
        group = []
        for at, (ref, where) in enumerate(parts):
            target = weights.at[slot] if where is None else weights.at[slot, where]
            group.append(pltpu.make_async_copy(ref, target, sems.at[2 * slot + at]))
            group[-1].start()
        copies.append(group)
    width = depth // 2
    mix[:, pl.ds(pl.multiple_of(core * width, 128), width)] = mix_mine[...]
    mix[:, pl.ds(pl.multiple_of((1 - core) * width, 128), width)] = mix_mate[...]
    started = jnp.where(me + outer > 0, 1.0, 0.0)
    groups = rows // POOL
    moment = jnp.zeros((groups, 1), jnp.float32)
    for slot, owner in enumerate(owners):
        for copy in copies[slot]:
            copy.wait()
        columns = pl.ds(pl.multiple_of(owner * shard, 128), shard)
        projected = jnp.dot(mix[...], weights[slot], preferred_element_type=jnp.float32)
        before = (edge[:, columns].astype(jnp.float32) + projected[:EXTRA]).astype(jnp.bfloat16)
        state = (stream[:, columns].astype(jnp.float32) + projected[EXTRA:]).astype(jnp.bfloat16)
        state_out[:, columns] = state
        before = before[EXTRA - POOL :].astype(jnp.float32) * started
        cells = jnp.concatenate([before, state.astype(jnp.float32)], axis=0)
        cells = cells.reshape(groups + 1, POOL, shard)
        tail = jnp.where(lax.broadcasted_iota(jnp.int32, cells.shape, 1) > 0, cells, 0.0)
        tail = jnp.sum(tail, axis=1)
        head = jnp.where(lax.broadcasted_iota(jnp.int32, cells.shape, 1) > 0, 0.0, cells)
        head = jnp.sum(head, axis=1)
        pooled = ((tail[:groups] + head[1:]) / POOL).astype(jnp.bfloat16)
        pooled_out[:, columns] = pooled
        pooled = pooled.astype(jnp.float32)
        wide[:, columns] = pooled
        moment = moment + jnp.sum(pooled * pooled, axis=-1, keepdims=True)
    factor = lax.rsqrt(moment / model_width + 1e-06)
    normed_out[...] = (wide[...] * factor * gain[...]).astype(jnp.bfloat16)


def fine_state_of(mixes, stream, edge, gain, pieces):
    rows, model_width = stream.shape
    devices = lax.axis_size("inner")
    depth, shard = pieces[0].shape
    groups = rows // POOL
    anywhere = pl.BlockSpec(memory_space=pl.ANY)
    inside = pl.BlockSpec(memory_space=pltpu.VMEM)
    return pl.pallas_call(
        functools.partial(state_kernel, (len(pieces),)),
        out_shape=(
            jax.ShapeDtypeStruct((rows, model_width), jnp.bfloat16),
            jax.ShapeDtypeStruct((groups, model_width), jnp.bfloat16),
            jax.ShapeDtypeStruct((groups, model_width), jnp.bfloat16),
        ),
        in_specs=[inside] * 5 + [anywhere] * len(pieces),
        out_specs=(inside,) * 3,
        scratch_shapes=[
            pltpu.VMEM((rows + EXTRA, depth), jnp.bfloat16),
            pltpu.VMEM((devices, depth, shard), jnp.bfloat16),
            pltpu.VMEM((groups, model_width), jnp.float32),
            pltpu.SemaphoreType.DMA((2 * devices,)),
        ],
        compiler_params=pltpu.CompilerParams(vmem_limit_bytes=24 * 1024 * 1024),
        cost_estimate=pl.CostEstimate(
            flops=2 * (rows + EXTRA) * depth * model_width,
            bytes_accessed=2 * depth * model_width + 4 * rows * model_width,
            transcendentals=groups,
        ),
        name="fine_state",
    )(*mixes, stream, edge, gain.reshape(1, model_width), *pieces)


def on_device(
    fine_input,
    fine_query,
    fine_key,
    fine_value,
    w_fine_out,
    norm_gain,
    w_query,
    w_key,
    w_value,
    w_coarse_out,
):
    tok_rows, model_width = fine_input.shape
    score_scale = 1.0 / math.sqrt(HE)
    edge = on_ahead(fine_input[tok_rows - EXTRA :], 1)
    pieces = shards_of_all(w_fine_out)
    mix_mine, mix_send = fine_attention(fine_query, fine_key, fine_value)
    mixes = (mix_mine, swapped_cores(mix_send))
    fine_state, pooled, normed = fine_state_of(mixes, fine_input, edge, norm_gain, pieces)
    pooled_wide = pooled.astype(jnp.float32)
    local_heads = w_query.shape[1] // HE
    head_width = local_heads * HE
    joined_weights = jnp.concatenate([w_query, w_key, w_value], axis=1)
    projections = jnp.dot(
        lax.all_gather(normed, "inner", axis=0, tiled=True),
        joined_weights,
        preferred_element_type=jnp.float32,
    ).astype(jnp.bfloat16)
    group_len = projections.shape[0]
    coarse_query = projections[:, :head_width].reshape(group_len, local_heads, HE)
    outer_index = lax.axis_index("outer")
    query_pos = outer_index * group_len + jnp.arange(group_len, dtype=jnp.int32)
    gathered = outer_gather(projections[:, head_width:])
    count = gathered.shape[0]
    block_keys = gathered[:, :head_width].reshape(count, local_heads, HE)
    block_values = gathered[:, head_width:].reshape(count, local_heads, HE)
    block_scores = (
        jnp.einsum("qhe,khe->hqk", coarse_query, block_keys, preferred_element_type=jnp.float32)
        * score_scale
    )
    key_pos = jnp.arange(count, dtype=jnp.int32)
    visible = (key_pos[None, :] <= query_pos[:, None])[None]
    block_masked = jnp.where(visible, block_scores, very_negative)
    new_max = jnp.max(block_masked, axis=-1)
    block_exp = jnp.where(visible, jnp.exp(block_scores - new_max[:, :, None]), 0.0)
    new_sum = jnp.sum(block_exp, axis=-1)
    contrib = jnp.einsum(
        "hqk,khe->hqe",
        block_exp.astype(jnp.bfloat16),
        block_values,
        preferred_element_type=jnp.float32,
    )
    coarse_mix = (
        jnp.transpose(contrib / new_sum[:, :, None], (1, 0, 2))
        .reshape(group_len, head_width)
        .astype(jnp.bfloat16)
    )
    head_total = summed_pieces(
        jnp.dot(coarse_mix, w_coarse_out, preferred_element_type=jnp.float32).astype(jnp.bfloat16)
    )
    coarse_out = (pooled_wide + head_total).astype(jnp.bfloat16)
    fine_groups = fine_state.reshape(tok_rows // POOL, POOL, model_width).astype(jnp.float32)
    lifted = fine_groups + coarse_out.astype(jnp.float32)[:, None, :]
    return lifted.reshape(tok_rows, model_width).astype(jnp.bfloat16)


def solution(mesh):
    placed = (
        P(("outer", "inner"), None),
        P(("outer", "inner"), None),
        P(("outer", "inner"), None),
        P(("outer", "inner"), None),
        P(None, "inner"),
        P(),
        P(None, "inner"),
        P(None, "inner"),
        P(None, "inner"),
        P("inner", None),
    )
    return jax.shard_map(
        on_device,
        mesh=mesh,
        in_specs=placed,
        out_specs=P(("outer", "inner"), None),
        check_vma=False,
    )
```

```python
import functools
import math

import jax
import jax.numpy as jnp
from jax import lax
from jax.experimental import pallas as pl
from jax.experimental.pallas import tpu as pltpu
from jax.sharding import PartitionSpec as P

HE = 128
WIN = 512
POOL = 8
EXTRA = 16
BOTH = ("outer", "inner")

very_negative = -1e30


def on_ahead(block, distance):
    count = lax.axis_size(BOTH)
    return lax.ppermute(block, BOTH, [(i, i + distance) for i in range(count - distance)])


def swapped_cores(block):
    count = lax.axis_size("inner")
    return lax.ppermute(block, "inner", [(i, i ^ 1) for i in range(count)])


def outer_mate(outer, inner):
    return outer ^ (1 if (inner >> 1) % 2 == 0 else 2)


def mate_bit(outer, inner):
    return jnp.where((inner >> 1) % 2 == 0, outer % 2, (outer >> 1) % 2)


def shards_of_all(shard):
    count, blocks = lax.axis_size("inner"), lax.axis_size("outer")
    me, outer = lax.axis_index("inner"), lax.axis_index("outer")
    half = shard.shape[0] // 2
    mates = [
        (o * count + i, outer_mate(o, i) * count + i) for o in range(blocks) for i in range(count)
    ]
    fetched = []
    for hop in range(2, count, 2):
        wanted = mate_bit(outer, (me + hop) % count)
        part = lax.dynamic_slice_in_dim(shard, wanted * half, half, 0)
        near = lax.ppermute(part, "inner", [(i, (i + hop) % count) for i in range(count)])
        fetched.append((near, lax.ppermute(near, BOTH, mates)))
    pieces = [shard, swapped_cores(shard)]
    for near, far in fetched:
        near_mate = swapped_cores(near)
        far_mate = swapped_cores(far)
        pieces += [near, far, near_mate, far_mate]
    return pieces


def outer_gather(block):
    count = lax.axis_size("outer")
    pairs = [[i, i + 1] for i in range(0, count, 2)]
    lines = [list(range(i, count, 2)) for i in range(2)]
    near = lax.all_gather(block, "outer", axis=0, tiled=True, axis_index_groups=pairs)
    return lax.all_gather(near, "outer", axis=0, tiled=True, axis_index_groups=lines)


def summed_pieces(block):
    count = lax.axis_size("inner")
    me = lax.axis_index("inner")
    parts = block.reshape(count, block.shape[0] // count, block.shape[1])
    own = lax.dynamic_index_in_dim(parts, me, 0, keepdims=False).astype(jnp.float32)
    for hop in range(1, count):
        piece = lax.dynamic_index_in_dim(parts, me ^ hop, 0, keepdims=False)
        own = own + lax.ppermute(piece, "inner", [(i, i ^ hop) for i in range(count)]).astype(
            jnp.float32
        )
    return own


def pack_kernel(takes, query, key, value, q_mate, k_mate, v_mate, *refs):
    blocks, (edges, sems) = refs[: len(takes)], refs[len(takes) :]
    rows = query.shape[0]
    width = edges.shape[2]
    core = lax.axis_index("inner") % 2
    own = pl.multiple_of(core * rows, 16)
    other = pl.multiple_of((1 - core) * rows, 16)
    columns = pl.ds(pl.multiple_of(core * width, 128), width)
    last = pl.ds(rows - EXTRA, EXTRA)
    moves = [
        (query.at[last, columns], edges.at[0]),
        (q_mate.at[last, columns], edges.at[1]),
    ]
    for ref, start, at in ((key, own, 0), (k_mate, other, 0), (value, own, 1), (v_mate, other, 1)):
        moves.append((ref.at[:, columns], blocks[0].at[pl.ds(start, rows), pl.ds(at * width, width)]))
    copies = [pltpu.make_async_copy(a, b, sems.at[i]) for i, (a, b) in enumerate(moves)]
    for copy in copies:
        copy.start()
    for copy in copies:
        copy.wait()
    ahead = 2 * rows
    blocks[0][ahead:, :width] = jnp.where(core == 1, edges[0], edges[1])
    blocks[0][ahead:, width:] = jnp.zeros((EXTRA, width), jnp.bfloat16)
    for take, block in zip(takes[1:], blocks[1:]):
        block[...] = blocks[0][ahead - take : ahead, :]


def attention_kernel(takes, query, key, value, q_mate, k_mate, v_mate, *refs):
    halos = refs[: len(takes)]
    mine_out, send_out, q_all, k_all, v_all, bias, sems = refs[len(takes) :]
    rows = query.shape[0]
    width = q_all.shape[1]
    core = lax.axis_index("inner") % 2
    chip = (lax.axis_index("outer") * lax.axis_size("inner") + lax.axis_index("inner")) // 2
    halo = sum(takes)
    copies = []

    def place(source, target):
        copy = pltpu.make_async_copy(source, target, sems.at[len(copies)])
        copy.start()
        copies.append(copy)

    own = pl.multiple_of(core * rows, 16)
    other = pl.multiple_of((1 - core) * rows, 16)
    columns = pl.ds(pl.multiple_of(core * width, 128), width)
    place(query.at[:, columns], q_all.at[pl.ds(EXTRA + own, rows)])
    place(key.at[:, columns], k_all.at[pl.ds(halo + own, rows)])
    place(value.at[:, columns], v_all.at[pl.ds(halo + own, rows)])
    place(q_mate.at[:, columns], q_all.at[pl.ds(EXTRA + other, rows)])
    place(k_mate.at[:, columns], k_all.at[pl.ds(halo + other, rows)])
    place(v_mate.at[:, columns], v_all.at[pl.ds(halo + other, rows)])
    place(halos[0].at[pl.ds(takes[0], EXTRA), pl.ds(0, width)], q_all.at[pl.ds(0, EXTRA)])
    start = halo
    for take, ref in zip(takes, halos):
        start -= take
        place(ref.at[pl.ds(0, take), pl.ds(0, width)], k_all.at[pl.ds(start, take)])
        place(ref.at[pl.ds(0, take), pl.ds(width, width)], v_all.at[pl.ds(start, take)])

    count, span = mine_out.shape[0], halo + rows
    row = lax.broadcasted_iota(jnp.int32, (count, span), 0) - EXTRA
    col = lax.broadcasted_iota(jnp.int32, (count, span), 1) - halo
    gap = row - col
    near = (gap >= 0) & (gap < WIN)
    scale = 1.0 / math.sqrt(HE)
    for copy in copies:
        copy.wait()
    for which, out in ((1 - core, send_out), (core, mine_out)):
        first = pl.multiple_of(which * rows, 16)
        bias[...] = jnp.where(near & (col + chip * 2 * rows + first >= 0), 0.0, very_negative)
        for head in range(width // HE):
            lanes = pl.ds(head * HE, HE)
            scores = lax.dot_general(
                q_all[pl.ds(first, count), lanes],
                k_all[pl.ds(first, span), lanes],
                (((1,), (1,)), ((), ())),
                preferred_element_type=jnp.float32,
            )
            masked = scores * scale + bias[...]
            top = jnp.max(masked, axis=-1, keepdims=True)
            weights = jnp.exp(masked - top)
            total = jnp.sum(weights, axis=-1, keepdims=True)
            summed = jnp.dot(
                weights.astype(jnp.bfloat16),
                v_all[pl.ds(first, span), lanes],
                preferred_element_type=jnp.float32,
            )
            out[:, lanes] = (summed / total).astype(jnp.bfloat16)


def fine_attention(fine_query, fine_key, fine_value):
    rows, full = fine_query.shape
    width = full // 2
    parts = (fine_query, fine_key, fine_value)
    mates = []
    for part in parts:
        mates.append(swapped_cores(part))
    left = -(-(WIN - 1 + EXTRA) // 16) * 16
    takes = []
    while left > 0:
        takes.append(min(left, 2 * rows))
        left -= takes[-1]
    anywhere = pl.BlockSpec(memory_space=pl.ANY)
    inside = pl.BlockSpec(memory_space=pltpu.VMEM)
    heights = [2 * rows + EXTRA] + takes[1:]
    blocks = pl.pallas_call(
        functools.partial(pack_kernel, tuple(takes)),
        out_shape=tuple(jax.ShapeDtypeStruct((h, full), jnp.bfloat16) for h in heights),
        in_specs=[anywhere] * 6,
        out_specs=(inside,) * len(takes),
        scratch_shapes=[
            pltpu.VMEM((2, EXTRA, width), jnp.bfloat16),
            pltpu.SemaphoreType.DMA((6,)),
        ],
        compiler_params=pltpu.CompilerParams(vmem_limit_bytes=8 * 1024 * 1024),
        cost_estimate=pl.CostEstimate(
            flops=0, bytes_accessed=8 * rows * full, transcendentals=0
        ),
        name="pack",
    )(*parts, *mates)
    halos = []
    for at, block in enumerate(blocks):
        halos.append(on_ahead(block, 2 * (at + 1)))
    count, halo = rows + EXTRA, sum(takes)
    out = jax.ShapeDtypeStruct((count, width), jnp.bfloat16)
    pairs = 4 * (width // HE) * count * (halo + rows)
    return pl.pallas_call(
        functools.partial(attention_kernel, tuple(takes)),
        out_shape=(out, out),
        in_specs=[anywhere] * (6 + len(takes)),
        out_specs=(pl.BlockSpec(memory_space=pltpu.VMEM),) * 2,
        scratch_shapes=[
            pltpu.VMEM((2 * rows + EXTRA, width), jnp.bfloat16),
            pltpu.VMEM((2 * rows + halo, width), jnp.bfloat16),
            pltpu.VMEM((2 * rows + halo, width), jnp.bfloat16),
            pltpu.VMEM((count, halo + rows), jnp.float32),
            pltpu.SemaphoreType.DMA((7 + 2 * len(takes),)),
        ],
        compiler_params=pltpu.CompilerParams(vmem_limit_bytes=24 * 1024 * 1024),
        cost_estimate=pl.CostEstimate(
            flops=2 * pairs * HE, bytes_accessed=6 * rows * full, transcendentals=pairs // 2
        ),
        name="fine_attention",
    )(*parts, *mates, *halos)


def state_kernel(counts, mix_mine, mix_mate, stream, edge, gain, *refs):
    pieces, refs = refs[: counts[0]], refs[counts[0] :]
    state_out, pooled_out, normed_out, mix, weights, wide, sems = refs
    rows, model_width = stream.shape
    devices = lax.axis_size("inner")
    shard = model_width // devices
    depth, half = weights.shape[1], weights.shape[1] // 2
    me, outer = lax.axis_index("inner"), lax.axis_index("outer")
    core = me % 2
    bit = jnp.where((me // 2) % 2 == 0, outer % 2, (outer // 2) % 2)
    first_half = pl.ds(pl.multiple_of(bit * half, 16), half)
    second_half = pl.ds(pl.multiple_of((1 - bit) * half, 16), half)
    slots = [[(pieces[0], None)], [(pieces[1], None)]]
    owners = [me, me + 1 - 2 * core]
    for hop in range(2, devices, 2):
        near, far, near_mate, far_mate = pieces[2 * hop - 2 : 2 * hop + 2]
        owner = lax.rem(me - hop + devices, devices)
        slots += [
            [(near, first_half), (far, second_half)],
            [(near_mate, first_half), (far_mate, second_half)],
        ]
        owners += [owner, owner + 1 - 2 * core]
    copies = []
    for slot, parts in enumerate(slots):
        group = []
        for at, (ref, where) in enumerate(parts):
            target = weights.at[slot] if where is None else weights.at[slot, where]
            group.append(pltpu.make_async_copy(ref, target, sems.at[2 * slot + at]))
            group[-1].start()
        copies.append(group)
    width = depth // 2
    mix[:, pl.ds(pl.multiple_of(core * width, 128), width)] = mix_mine[...]
    mix[:, pl.ds(pl.multiple_of((1 - core) * width, 128), width)] = mix_mate[...]
    started = jnp.where(me + outer > 0, 1.0, 0.0)
    groups = rows // POOL
    moment = jnp.zeros((groups, 1), jnp.float32)
    for slot, owner in enumerate(owners):
        for copy in copies[slot]:
            copy.wait()
        columns = pl.ds(pl.multiple_of(owner * shard, 128), shard)
        projected = jnp.dot(mix[...], weights[slot], preferred_element_type=jnp.float32)
        before = (edge[:, columns].astype(jnp.float32) + projected[:EXTRA]).astype(jnp.bfloat16)
        state = (stream[:, columns].astype(jnp.float32) + projected[EXTRA:]).astype(jnp.bfloat16)
        state_out[:, columns] = state
        before = before[EXTRA - POOL :].astype(jnp.float32) * started
        cells = jnp.concatenate([before, state.astype(jnp.float32)], axis=0)
        cells = cells.reshape(groups + 1, POOL, shard)
        tail = jnp.where(lax.broadcasted_iota(jnp.int32, cells.shape, 1) > 0, cells, 0.0)
        tail = jnp.sum(tail, axis=1)
        head = jnp.where(lax.broadcasted_iota(jnp.int32, cells.shape, 1) > 0, 0.0, cells)
        head = jnp.sum(head, axis=1)
        pooled = ((tail[:groups] + head[1:]) / POOL).astype(jnp.bfloat16)
        pooled_out[:, columns] = pooled
        pooled = pooled.astype(jnp.float32)
        wide[:, columns] = pooled
        moment = moment + jnp.sum(pooled * pooled, axis=-1, keepdims=True)
    factor = lax.rsqrt(moment / model_width + 1e-06)
    normed_out[...] = (wide[...] * factor * gain[...]).astype(jnp.bfloat16)


def fine_state_of(mixes, stream, edge, gain, pieces):
    rows, model_width = stream.shape
    devices = lax.axis_size("inner")
    depth, shard = pieces[0].shape
    groups = rows // POOL
    anywhere = pl.BlockSpec(memory_space=pl.ANY)
    inside = pl.BlockSpec(memory_space=pltpu.VMEM)
    return pl.pallas_call(
        functools.partial(state_kernel, (len(pieces),)),
        out_shape=(
            jax.ShapeDtypeStruct((rows, model_width), jnp.bfloat16),
            jax.ShapeDtypeStruct((groups, model_width), jnp.bfloat16),
            jax.ShapeDtypeStruct((groups, model_width), jnp.bfloat16),
        ),
        in_specs=[inside] * 5 + [anywhere] * len(pieces),
        out_specs=(inside,) * 3,
        scratch_shapes=[
            pltpu.VMEM((rows + EXTRA, depth), jnp.bfloat16),
            pltpu.VMEM((devices, depth, shard), jnp.bfloat16),
            pltpu.VMEM((groups, model_width), jnp.float32),
            pltpu.SemaphoreType.DMA((2 * devices,)),
        ],
        compiler_params=pltpu.CompilerParams(vmem_limit_bytes=24 * 1024 * 1024),
        cost_estimate=pl.CostEstimate(
            flops=2 * (rows + EXTRA) * depth * model_width,
            bytes_accessed=2 * depth * model_width + 4 * rows * model_width,
            transcendentals=groups,
        ),
        name="fine_state",
    )(*mixes, stream, edge, gain.reshape(1, model_width), *pieces)


def on_device(
    fine_input,
    fine_query,
    fine_key,
    fine_value,
    w_fine_out,
    norm_gain,
    w_query,
    w_key,
    w_value,
    w_coarse_out,
):
    tok_rows, model_width = fine_input.shape
    score_scale = 1.0 / math.sqrt(HE)
    edge = on_ahead(fine_input[tok_rows - EXTRA :], 1)
    pieces = shards_of_all(w_fine_out)
    mix_mine, mix_send = fine_attention(fine_query, fine_key, fine_value)
    mixes = (mix_mine, swapped_cores(mix_send))
    fine_state, pooled, normed = fine_state_of(mixes, fine_input, edge, norm_gain, pieces)
    pooled_wide = pooled.astype(jnp.float32)
    local_heads = w_query.shape[1] // HE
    head_width = local_heads * HE
    joined_weights = jnp.concatenate([w_query, w_key, w_value], axis=1)
    projections = jnp.dot(
        lax.all_gather(normed, "inner", axis=0, tiled=True),
        joined_weights,
        preferred_element_type=jnp.float32,
    ).astype(jnp.bfloat16)
    group_len = projections.shape[0]
    coarse_query = projections[:, :head_width].reshape(group_len, local_heads, HE)
    outer_index = lax.axis_index("outer")
    query_pos = outer_index * group_len + jnp.arange(group_len, dtype=jnp.int32)
    gathered = outer_gather(projections[:, head_width:])
    count = gathered.shape[0]
    block_keys = gathered[:, :head_width].reshape(count, local_heads, HE)
    block_values = gathered[:, head_width:].reshape(count, local_heads, HE)
    block_scores = (
        jnp.einsum("qhe,khe->hqk", coarse_query, block_keys, preferred_element_type=jnp.float32)
        * score_scale
    )
    key_pos = jnp.arange(count, dtype=jnp.int32)
    visible = (key_pos[None, :] <= query_pos[:, None])[None]
    block_masked = jnp.where(visible, block_scores, very_negative)
    new_max = jnp.max(block_masked, axis=-1)
    block_exp = jnp.where(visible, jnp.exp(block_scores - new_max[:, :, None]), 0.0)
    new_sum = jnp.sum(block_exp, axis=-1)
    contrib = jnp.einsum(
        "hqk,khe->hqe",
        block_exp.astype(jnp.bfloat16),
        block_values,
        preferred_element_type=jnp.float32,
    )
    coarse_mix = (
        jnp.transpose(contrib / new_sum[:, :, None], (1, 0, 2))
        .reshape(group_len, head_width)
        .astype(jnp.bfloat16)
    )
    head_total = summed_pieces(
        jnp.dot(coarse_mix, w_coarse_out, preferred_element_type=jnp.float32).astype(jnp.bfloat16)
    )
    coarse_out = (pooled_wide + head_total).astype(jnp.bfloat16)
    fine_groups = fine_state.reshape(tok_rows // POOL, POOL, model_width).astype(jnp.float32)
    lifted = fine_groups + coarse_out.astype(jnp.float32)[:, None, :]
    return lifted.reshape(tok_rows, model_width).astype(jnp.bfloat16)


def solution(mesh):
    placed = (
        P(("outer", "inner"), None),
        P(("outer", "inner"), None),
        P(("outer", "inner"), None),
        P(("outer", "inner"), None),
        P(None, "inner"),
        P(),
        P(None, "inner"),
        P(None, "inner"),
        P(None, "inner"),
        P("inner", None),
    )

    return jax.shard_map(
        on_device,
        mesh=mesh,
        in_specs=placed,
        out_specs=P(("outer", "inner"), None),
        check_vma=False,
    )
```

```python
import functools
import math

import jax
import jax.numpy as jnp
from jax import lax
from jax.experimental import pallas as pl
from jax.experimental.pallas import tpu as pltpu
from jax.sharding import PartitionSpec as P

HE = 128
WIN = 512
POOL = 8
EXTRA = 16
BOTH = ("outer", "inner")

very_negative = -1e30


def on_ahead(block, distance):
    count = lax.axis_size(BOTH)
    return lax.ppermute(block, BOTH, [(i, i + distance) for i in range(count - distance)])


def swapped_cores(block):
    count = lax.axis_size("inner")
    return lax.ppermute(block, "inner", [(i, i ^ 1) for i in range(count)])


def outer_mate(outer, inner):
    return outer ^ (1 if (inner >> 1) % 2 == 0 else 2)


def mate_bit(outer, inner):
    return jnp.where((inner >> 1) % 2 == 0, outer % 2, (outer >> 1) % 2)


def shards_of_all(shard):
    count, blocks = lax.axis_size("inner"), lax.axis_size("outer")
    me, outer = lax.axis_index("inner"), lax.axis_index("outer")
    half = shard.shape[0] // 2
    mates = [
        (o * count + i, outer_mate(o, i) * count + i) for o in range(blocks) for i in range(count)
    ]
    fetched = []
    for hop in range(2, count, 2):
        wanted = mate_bit(outer, (me + hop) % count)
        part = lax.dynamic_slice_in_dim(shard, wanted * half, half, 0)
        near = lax.ppermute(part, "inner", [(i, (i + hop) % count) for i in range(count)])
        fetched.append((near, lax.ppermute(near, BOTH, mates)))
    pieces = [shard, swapped_cores(shard)]
    for near, far in fetched:
        near_mate = swapped_cores(near)
        far_mate = swapped_cores(far)
        pieces += [near, far, near_mate, far_mate]
    return pieces


def outer_pieces(block):
    count = lax.axis_size("outer")
    mate = lax.ppermute(block, "outer", [(i, i ^ 1) for i in range(count)])
    both = jnp.concatenate([block, mate], axis=0)
    return [both] + [
        lax.ppermute(both, "outer", [(i, i ^ hop) for i in range(count)])
        for hop in range(2, count, 2)
    ]


def coarse_kernel(length, projections, w_out, *refs):
    pieces, out = refs[:-1], refs[-1]
    width = w_out.shape[0]
    outer = lax.axis_index("outer")
    scale = 1.0 / math.sqrt(HE)
    row = lax.broadcasted_iota(jnp.int32, (length, 2 * length), 0) + outer * length
    col = lax.broadcasted_iota(jnp.int32, (length, 2 * length), 1)
    second = col >= length
    col = jnp.where(second, col - length, col)
    mixes = []
    for head in range(width // HE):
        query = projections[:, head * HE : (head + 1) * HE]
        top = total = summed = None
        for at, piece in enumerate(pieces):
            block = outer ^ (2 * at)
            position = col + jnp.where(second, block ^ 1, block) * length
            scores = lax.dot_general(
                query,
                piece[:, head * HE : (head + 1) * HE],
                (((1,), (1,)), ((), ())),
                preferred_element_type=jnp.float32,
            )
            scores = jnp.where(position <= row, scores * scale, very_negative)
            high = jnp.max(scores, axis=-1, keepdims=True)
            if at:
                high = jnp.maximum(high, top)
            weights = jnp.exp(scores - high)
            part = jnp.sum(weights, axis=-1, keepdims=True)
            mixed = jnp.dot(
                weights.astype(jnp.bfloat16),
                piece[:, width + head * HE : width + (head + 1) * HE],
                preferred_element_type=jnp.float32,
            )
            if at:
                shrink = jnp.exp(top - high)
                part, mixed = part + total * shrink, mixed + summed * shrink
            top, total, summed = high, part, mixed
        mixes.append((summed / total).astype(jnp.bfloat16))
    mix = mixes[0] if len(mixes) == 1 else jnp.concatenate(mixes, axis=1)
    out[...] = jnp.dot(mix, w_out[...], preferred_element_type=jnp.float32).astype(jnp.bfloat16)


def coarse_partial(projections, w_coarse_out, pieces):
    length = projections.shape[0]
    inside = pl.BlockSpec(memory_space=pltpu.VMEM)
    keys = sum(piece.shape[0] for piece in pieces)
    width, model_width = w_coarse_out.shape
    return pl.pallas_call(
        functools.partial(coarse_kernel, length),
        out_shape=jax.ShapeDtypeStruct((length, model_width), jnp.bfloat16),
        in_specs=[inside] * (2 + len(pieces)),
        out_specs=inside,
        compiler_params=pltpu.CompilerParams(vmem_limit_bytes=8 * 1024 * 1024 + 8 * keys * width),
        cost_estimate=pl.CostEstimate(
            flops=4 * length * keys * width + 2 * length * width * model_width,
            bytes_accessed=4 * keys * width + 2 * (width + length) * model_width,
            transcendentals=length * keys,
        ),
        name="coarse",
    )(projections, w_coarse_out, *pieces)


def summed_pieces(block):
    count = lax.axis_size("inner")
    me = lax.axis_index("inner")
    parts = block.reshape(count, block.shape[0] // count, block.shape[1])
    own = lax.dynamic_index_in_dim(parts, me, 0, keepdims=False).astype(jnp.float32)
    for hop in range(1, count):
        piece = lax.dynamic_index_in_dim(parts, me ^ hop, 0, keepdims=False)
        own = own + lax.ppermute(piece, "inner", [(i, i ^ hop) for i in range(count)]).astype(
            jnp.float32
        )
    return own


def pack_kernel(takes, stream, query, key, value, q_mate, k_mate, v_mate, *refs):
    blocks, (edge_out, edges, sems) = refs[: len(takes)], refs[len(takes) :]
    rows = query.shape[0]
    width = edges.shape[2]
    core = lax.axis_index("inner") % 2
    own = pl.multiple_of(core * rows, 16)
    other = pl.multiple_of((1 - core) * rows, 16)
    columns = pl.ds(pl.multiple_of(core * width, 128), width)
    last = pl.ds(rows - EXTRA, EXTRA)
    moves = [
        (query.at[last, columns], edges.at[0]),
        (q_mate.at[last, columns], edges.at[1]),
        (stream.at[last], edge_out),
    ]
    for ref, start, at in ((key, own, 0), (k_mate, other, 0), (value, own, 1), (v_mate, other, 1)):
        moves.append((ref.at[:, columns], blocks[0].at[pl.ds(start, rows), pl.ds(at * width, width)]))
    copies = [pltpu.make_async_copy(a, b, sems.at[i]) for i, (a, b) in enumerate(moves)]
    for copy in copies:
        copy.start()
    for copy in copies:
        copy.wait()
    ahead = 2 * rows
    blocks[0][ahead:, :width] = jnp.where(core == 1, edges[0], edges[1])
    blocks[0][ahead:, width:] = jnp.zeros((EXTRA, width), jnp.bfloat16)
    for take, block in zip(takes[1:], blocks[1:]):
        block[...] = blocks[0][ahead - take : ahead, :]


def attention_kernel(takes, query, key, value, q_mate, k_mate, v_mate, *refs):
    halos = refs[: len(takes)]
    mine_out, send_out, q_all, k_all, v_all, bias, sems = refs[len(takes) :]
    rows = query.shape[0]
    width = q_all.shape[1]
    core = lax.axis_index("inner") % 2
    chip = (lax.axis_index("outer") * lax.axis_size("inner") + lax.axis_index("inner")) // 2
    halo = sum(takes)
    copies = []

    def place(source, target):
        copy = pltpu.make_async_copy(source, target, sems.at[len(copies)])
        copy.start()
        copies.append(copy)

    own = pl.multiple_of(core * rows, 16)
    other = pl.multiple_of((1 - core) * rows, 16)
    columns = pl.ds(pl.multiple_of(core * width, 128), width)
    place(query.at[:, columns], q_all.at[pl.ds(EXTRA + own, rows)])
    place(key.at[:, columns], k_all.at[pl.ds(halo + own, rows)])
    place(value.at[:, columns], v_all.at[pl.ds(halo + own, rows)])
    place(q_mate.at[:, columns], q_all.at[pl.ds(EXTRA + other, rows)])
    place(k_mate.at[:, columns], k_all.at[pl.ds(halo + other, rows)])
    place(v_mate.at[:, columns], v_all.at[pl.ds(halo + other, rows)])
    place(halos[0].at[pl.ds(takes[0], EXTRA), pl.ds(0, width)], q_all.at[pl.ds(0, EXTRA)])
    start = halo
    for take, ref in zip(takes, halos):
        start -= take
        place(ref.at[pl.ds(0, take), pl.ds(0, width)], k_all.at[pl.ds(start, take)])
        place(ref.at[pl.ds(0, take), pl.ds(width, width)], v_all.at[pl.ds(start, take)])

    count, span = mine_out.shape[0], halo + rows
    row = lax.broadcasted_iota(jnp.int32, (count, span), 0) - EXTRA
    col = lax.broadcasted_iota(jnp.int32, (count, span), 1) - halo
    gap = row - col
    near = (gap >= 0) & (gap < WIN)
    scale = 1.0 / math.sqrt(HE)
    for copy in copies:
        copy.wait()
    for which, out in ((1 - core, send_out), (core, mine_out)):
        first = pl.multiple_of(which * rows, 16)
        bias[...] = jnp.where(near & (col + chip * 2 * rows + first >= 0), 0.0, very_negative)
        for head in range(width // HE):
            lanes = pl.ds(head * HE, HE)
            scores = lax.dot_general(
                q_all[pl.ds(first, count), lanes],
                k_all[pl.ds(first, span), lanes],
                (((1,), (1,)), ((), ())),
                preferred_element_type=jnp.float32,
            )
            masked = scores * scale + bias[...]
            top = jnp.max(masked, axis=-1, keepdims=True)
            weights = jnp.exp(masked - top)
            total = jnp.sum(weights, axis=-1, keepdims=True)
            summed = jnp.dot(
                weights.astype(jnp.bfloat16),
                v_all[pl.ds(first, span), lanes],
                preferred_element_type=jnp.float32,
            )
            out[:, lanes] = (summed / total).astype(jnp.bfloat16)


def fine_attention(fine_input, fine_query, fine_key, fine_value):
    rows, full = fine_query.shape
    width = full // 2
    parts = (fine_query, fine_key, fine_value)
    mates = []
    for part in parts:
        mates.append(swapped_cores(part))
    left = -(-(WIN - 1 + EXTRA) // 16) * 16
    takes = []
    while left > 0:
        takes.append(min(left, 2 * rows))
        left -= takes[-1]
    anywhere = pl.BlockSpec(memory_space=pl.ANY)
    inside = pl.BlockSpec(memory_space=pltpu.VMEM)
    heights = [2 * rows + EXTRA] + takes[1:]
    shapes = [(h, full) for h in heights] + [(EXTRA, fine_input.shape[1])]
    *blocks, edge = pl.pallas_call(
        functools.partial(pack_kernel, tuple(takes)),
        out_shape=tuple(jax.ShapeDtypeStruct(shape, jnp.bfloat16) for shape in shapes),
        in_specs=[anywhere] * 7,
        out_specs=(inside,) * len(shapes),
        scratch_shapes=[
            pltpu.VMEM((2, EXTRA, width), jnp.bfloat16),
            pltpu.SemaphoreType.DMA((7,)),
        ],
        compiler_params=pltpu.CompilerParams(vmem_limit_bytes=4 * 1024 * 1024),
        cost_estimate=pl.CostEstimate(
            flops=0, bytes_accessed=8 * rows * full, transcendentals=0
        ),
        name="pack",
    )(fine_input, *parts, *mates)
    edge = on_ahead(edge, 1)
    halos = []
    for at, block in enumerate(blocks):
        halos.append(on_ahead(block, 2 * (at + 1)))
    count, halo = rows + EXTRA, sum(takes)
    out = jax.ShapeDtypeStruct((count, width), jnp.bfloat16)
    pairs = 4 * (width // HE) * count * (halo + rows)
    mixes = pl.pallas_call(
        functools.partial(attention_kernel, tuple(takes)),
        out_shape=(out, out),
        in_specs=[anywhere] * (6 + len(takes)),
        out_specs=(pl.BlockSpec(memory_space=pltpu.VMEM),) * 2,
        scratch_shapes=[
            pltpu.VMEM((2 * rows + EXTRA, width), jnp.bfloat16),
            pltpu.VMEM((2 * rows + halo, width), jnp.bfloat16),
            pltpu.VMEM((2 * rows + halo, width), jnp.bfloat16),
            pltpu.VMEM((count, halo + rows), jnp.float32),
            pltpu.SemaphoreType.DMA((7 + 2 * len(takes),)),
        ],
        compiler_params=pltpu.CompilerParams(vmem_limit_bytes=10 * 1024 * 1024),
        cost_estimate=pl.CostEstimate(
            flops=2 * pairs * HE, bytes_accessed=6 * rows * full, transcendentals=pairs // 2
        ),
        name="fine_attention",
    )(*parts, *mates, *halos)
    return mixes, edge


def state_kernel(counts, mix_mine, mix_mate, stream, edge, gain, *refs):
    pieces, refs = refs[: counts[0]], refs[counts[0] :]
    state_out, pooled_out, normed_out, mix, weights, wide, rows_in, edge_in, sems = refs
    rows, model_width = stream.shape
    devices = lax.axis_size("inner")
    shard = model_width // devices
    depth, half = weights.shape[1], weights.shape[1] // 2
    me, outer = lax.axis_index("inner"), lax.axis_index("outer")
    core = me % 2
    bit = jnp.where((me // 2) % 2 == 0, outer % 2, (outer // 2) % 2)
    first_half = pl.ds(pl.multiple_of(bit * half, 16), half)
    second_half = pl.ds(pl.multiple_of((1 - bit) * half, 16), half)
    slots = [[(pieces[0], None)], [(pieces[1], None)]]
    owners = [me, me + 1 - 2 * core]
    for hop in range(2, devices, 2):
        near, far, near_mate, far_mate = pieces[2 * hop - 2 : 2 * hop + 2]
        owner = lax.rem(me - hop + devices, devices)
        slots += [
            [(near, first_half), (far, second_half)],
            [(near_mate, first_half), (far_mate, second_half)],
        ]
        owners += [owner, owner + 1 - 2 * core]
    copies = []
    for slot, parts in enumerate(slots):
        group = []
        for at, (ref, where) in enumerate(parts):
            target = weights.at[slot] if where is None else weights.at[slot, where]
            group.append(pltpu.make_async_copy(ref, target, sems.at[2 * slot + at]))
            group[-1].start()
        copies.append(group)
    width = depth // 2
    kept = pl.ds(pl.multiple_of(core * width, 128), width)
    given = pl.ds(pl.multiple_of((1 - core) * width, 128), width)
    moves = (
        (mix_mine, mix.at[:, kept]),
        (mix_mate, mix.at[:, given]),
        (edge, edge_in),
        (stream, rows_in),
    )
    loads = [
        pltpu.make_async_copy(a, b, sems.at[2 * devices + i]) for i, (a, b) in enumerate(moves)
    ]
    for load in loads:
        load.start()
    for load in loads:
        load.wait()
    started = jnp.where(me + outer > 0, 1.0, 0.0)
    groups = rows // POOL
    moment = jnp.zeros((groups, 1), jnp.float32)
    for slot, owner in enumerate(owners):
        for copy in copies[slot]:
            copy.wait()
        columns = pl.ds(pl.multiple_of(owner * shard, 128), shard)
        projected = jnp.dot(mix[...], weights[slot], preferred_element_type=jnp.float32)
        before = (edge_in[:, columns].astype(jnp.float32) + projected[:EXTRA]).astype(jnp.bfloat16)
        state = (rows_in[:, columns].astype(jnp.float32) + projected[EXTRA:]).astype(jnp.bfloat16)
        state_out[:, columns] = state
        before = before[EXTRA - POOL :].astype(jnp.float32) * started
        cells = jnp.concatenate([before, state.astype(jnp.float32)], axis=0)
        cells = cells.reshape(groups + 1, POOL, shard)
        tail = jnp.where(lax.broadcasted_iota(jnp.int32, cells.shape, 1) > 0, cells, 0.0)
        tail = jnp.sum(tail, axis=1)
        head = jnp.where(lax.broadcasted_iota(jnp.int32, cells.shape, 1) > 0, 0.0, cells)
        head = jnp.sum(head, axis=1)
        pooled = ((tail[:groups] + head[1:]) / POOL).astype(jnp.bfloat16)
        pooled_out[:, columns] = pooled
        pooled = pooled.astype(jnp.float32)
        wide[:, columns] = pooled
        moment = moment + jnp.sum(pooled * pooled, axis=-1, keepdims=True)
    factor = lax.rsqrt(moment / model_width + 1e-06)
    normed_out[...] = (wide[...] * factor * gain[...]).astype(jnp.bfloat16)


def fine_state_of(mixes, stream, edge, gain, pieces):
    rows, model_width = stream.shape
    devices = lax.axis_size("inner")
    depth, shard = pieces[0].shape
    groups = rows // POOL
    anywhere = pl.BlockSpec(memory_space=pl.ANY)
    inside = pl.BlockSpec(memory_space=pltpu.VMEM)
    return pl.pallas_call(
        functools.partial(state_kernel, (len(pieces),)),
        out_shape=(
            jax.ShapeDtypeStruct((rows, model_width), jnp.bfloat16),
            jax.ShapeDtypeStruct((groups, model_width), jnp.bfloat16),
            jax.ShapeDtypeStruct((groups, model_width), jnp.bfloat16),
        ),
        in_specs=[anywhere] * 4 + [inside] + [anywhere] * len(pieces),
        out_specs=(inside,) * 3,
        scratch_shapes=[
            pltpu.VMEM((rows + EXTRA, depth), jnp.bfloat16),
            pltpu.VMEM((devices, depth, shard), jnp.bfloat16),
            pltpu.VMEM((groups, model_width), jnp.float32),
            pltpu.VMEM((rows, model_width), jnp.bfloat16),
            pltpu.VMEM((EXTRA, model_width), jnp.bfloat16),
            pltpu.SemaphoreType.DMA((2 * devices + 4,)),
        ],
        compiler_params=pltpu.CompilerParams(vmem_limit_bytes=14 * 1024 * 1024),
        cost_estimate=pl.CostEstimate(
            flops=2 * (rows + EXTRA) * depth * model_width,
            bytes_accessed=2 * depth * model_width + 4 * rows * model_width,
            transcendentals=groups,
        ),
        name="fine_state",
    )(*mixes, stream, edge, gain.reshape(1, model_width), *pieces)


def on_device(
    fine_input,
    fine_query,
    fine_key,
    fine_value,
    w_fine_out,
    norm_gain,
    w_query,
    w_key,
    w_value,
    w_coarse_out,
):
    tok_rows, model_width = fine_input.shape
    pieces = shards_of_all(w_fine_out)
    (mix_mine, mix_send), edge = fine_attention(fine_input, fine_query, fine_key, fine_value)
    mixes = (mix_mine, swapped_cores(mix_send))
    fine_state, pooled, normed = fine_state_of(mixes, fine_input, edge, norm_gain, pieces)
    pooled_wide = pooled.astype(jnp.float32)
    local_heads = w_query.shape[1] // HE
    head_width = local_heads * HE
    joined_weights = jnp.concatenate([w_query, w_key, w_value], axis=1)
    projections = jnp.dot(
        lax.all_gather(normed, "inner", axis=0, tiled=True),
        joined_weights,
        preferred_element_type=jnp.float32,
    ).astype(jnp.bfloat16)
    partial = coarse_partial(
        projections[:, :head_width], w_coarse_out, outer_pieces(projections[:, head_width:])
    )
    head_total = summed_pieces(partial)
    coarse_out = (pooled_wide + head_total).astype(jnp.bfloat16)
    fine_groups = fine_state.reshape(tok_rows // POOL, POOL, model_width).astype(jnp.float32)
    lifted = fine_groups + coarse_out.astype(jnp.float32)[:, None, :]
    return lifted.reshape(tok_rows, model_width).astype(jnp.bfloat16)


def solution(mesh):
    placed = (
        P(("outer", "inner"), None),
        P(("outer", "inner"), None),
        P(("outer", "inner"), None),
        P(("outer", "inner"), None),
        P(None, "inner"),
        P(),
        P(None, "inner"),
        P(None, "inner"),
        P(None, "inner"),
        P("inner", None),
    )

    return jax.shard_map(
        on_device,
        mesh=mesh,
        in_specs=placed,
        out_specs=P(("outer", "inner"), None),
        check_vma=False,
    )
```
